512 devices in a mesh: pix: 64 (over z, y_lo, core), tm: 8 (over y_hi, x).
Axes of the slice: x: 4, y: 4 (y_hi: 2, y_lo: 2; y = y_hi * 2 + y_lo), z: 16, core: 2. Of those that a mesh axis runs over, the one named last changes fastest.
Arguments:
- signal: bfloat16 [16384, 16, 256], P('pix', 'tm'), may hold values from -6 to 6
- lap_tiles: bfloat16 [256, 9, 64, 64], P('pix'), may hold values from -0.25 to 0.25
- neighbours: int32 [256, 9], replicated, may hold values from 0 to 255, as said below
- cheb_weight: bfloat16 [3, 256, 256], replicated, may hold values from -0.21875 to 0.21875
- norm_gain: float32 [256], replicated, may hold values from 0.25 to 1.75
- w_query: bfloat16 [256, 256], replicated, may hold values from -6.5 to 6.5
- w_key: bfloat16 [256, 256], replicated, may hold values from -0.375 to 0.375
- w_value: bfloat16 [256, 256], replicated, may hold values from -0.375 to 0.375
- w_out: bfloat16 [256, 256], replicated, may hold values from -0.375 to 0.375
Outputs:
- result: bfloat16 [16384, 16, 256], P('pix', 'tm')
The draws below stay inside these ranges and needn't reach their ends.
Inputs may be any that keep to these rules, and one draw needn't show every extreme that they name: `neighbours`: row g lists blocks g - 2, g - 1, g, g + 1, g + 2 in its first five entries (g itself where one of them does not exist); each of the other four entries is one of those five.
All inputs are finite; a program needn't handle non-finite values.
Results may differ from the reference program's by a relative error of at most 0.017.
Values may be sent and summed in bfloat16 or wider, within the bound.
A program may use at most 64 MiB of HBM per device.

```python
import math
import jax
import jax.numpy as jnp
from jax import lax

C = 256
HEADS = 8
B = 64
NB = 9
PIX = 16384
TIMES = 16
NBLKS = 256


def draw_neighbours(key, part):
    base = jnp.arange(NBLKS, dtype=jnp.int32)
    last_block = NBLKS - 1
    columns = []
    for delta in (-2, -1, 0, 1, 2):
        moved = base + delta
        inside = jnp.logical_and(moved >= 0, moved <= last_block)
        columns.append(jnp.where(inside, moved, base))
    for extra in range(4):
        offset = jax.random.randint(jax.random.fold_in(key, 21 + extra), (NBLKS,), -2, 3, dtype=jnp.int32)
        moved = base + offset
        inside = jnp.logical_and(moved >= 0, moved <= last_block)
        columns.append(jnp.where(inside, moved, base))
    return jnp.stack(columns, axis=1).astype(jnp.int32)


def draw_w_query(key, part):
    key_factor = jax.random.fold_in(key, 11)
    key_entry = jax.random.fold_in(key, 12)
    spread = jax.random.uniform(key_factor, (HEADS,), jnp.float32)
    factor = jnp.exp(math.log(0.7) + spread * (math.log(2.5) - math.log(0.7)))
    entries = jax.random.truncated_normal(key_entry, -3.0, 3.0, (C, C), jnp.float32)
    column_scale = jnp.repeat(factor, C // HEADS)
    return (entries * column_scale[None, :] / math.sqrt(C)).astype(jnp.bfloat16)


def block_levels(key, shape, split, smallest, top_value):
    factor_of, own = 1.0, jax.random.fold_in(key, 6)
    for axis_at, blocks in split:
        heights = jnp.exp(jax.random.uniform(jax.random.fold_in(own, axis_at), (blocks,), jnp.float32, smallest / len(split), top_value / len(split)))
        factor_of = factor_of * jnp.repeat(heights, shape[axis_at] // blocks).reshape([-1 if axis == axis_at else 1 for axis in range(len(shape))])
    return factor_of


def scatter_about(key, dims, deviation, bound, split=(), kind=jnp.bfloat16):
    loudness = block_levels(key, dims, split, -0.22, 0.18) if split else 1.0
    drawn = jax.random.normal(key, dims, jnp.float32) * deviation * loudness
    return jnp.minimum(jnp.maximum(drawn, -bound), bound).astype(kind)


def setup_inputs(seed: int = 0) -> dict:
    seeds = jax.random.split(jax.random.key(seed), 10)
    signal = scatter_about(seeds[0], (PIX, TIMES, C), 1.0, 6.0, ((0, 64), (1, 8)))
    lap_tiles = scatter_about(seeds[1], (NBLKS, NB, B, B), (NB * B) ** -0.5, 0.25, ((0, 64),))
    neighbours = draw_neighbours(jax.random.fold_in(seeds[9], 71), 0)
    cheb_weight = scatter_about(seeds[3], (3, C, C), (3 * C) ** -0.5, 0.21875)
    norm_gain = jnp.clip(1.0 + 0.15 * jax.random.normal(seeds[4], (C,), jnp.float32), 0.25, 1.75)
    w_query = draw_w_query(jax.random.fold_in(seeds[9], 71), 0)
    w_key = scatter_about(seeds[6], (C, C), C ** -0.5, 0.375)
    w_value = scatter_about(seeds[7], (C, C), C ** -0.5, 0.375)
    w_out = scatter_about(seeds[8], (C, C), C ** -0.5, 0.375)
    return {"signal": signal, "lap_tiles": lap_tiles, "neighbours": neighbours, "cheb_weight": cheb_weight, "norm_gain": norm_gain, "w_query": w_query, "w_key": w_key, "w_value": w_value, "w_out": w_out}


def laplace(lap_tiles, neighbours, source, minus):

    def one_block(index):
        summed = jnp.zeros((B, source.shape[2]), jnp.float32)
        for slot in range(NB):
            chosen = source[neighbours[index, slot]]
            summed = summed + jnp.dot(lap_tiles[index, slot], chosen, preferred_element_type=jnp.float32)
        if minus is None:
            return summed.astype(jnp.bfloat16)
        return (2.0 * summed - minus[index].astype(jnp.float32)).astype(jnp.bfloat16)
    return lax.map(one_block, jnp.arange(NBLKS, dtype=jnp.int32))

def attend(mixed, norm_gain, w_query, w_key, w_value, w_out):
    count, times, channels = mixed.shape
    head_dim = channels // HEADS
    flat = mixed.reshape(count * times, channels).astype(jnp.float32)
    scaling = lax.rsqrt(lax.optimization_barrier(jnp.mean(flat * flat, axis=1, keepdims=True)) + 1e-06)
    normed = (flat * scaling * norm_gain.astype(jnp.float32)[None, :]).astype(jnp.bfloat16)
    query = jnp.dot(normed, w_query, preferred_element_type=jnp.float32).astype(jnp.bfloat16)
    keys = jnp.dot(normed, w_key, preferred_element_type=jnp.float32).astype(jnp.bfloat16)
    values = jnp.dot(normed, w_value, preferred_element_type=jnp.float32).astype(jnp.bfloat16)
    query = query.reshape(count, times, HEADS, head_dim).astype(jnp.float32)
    keys = keys.reshape(count, times, HEADS, head_dim).astype(jnp.float32)
    values = values.reshape(count, times, HEADS, head_dim).astype(jnp.float32)
    scores = jnp.einsum('pshd,pthd->phst', query, keys) / math.sqrt(head_dim)
    weights = jax.nn.softmax(scores, axis=-1).astype(jnp.bfloat16)
    attended = jnp.einsum('phst,pthd->pshd', weights.astype(jnp.float32), values).astype(jnp.bfloat16)
    attended = attended.reshape(count * times, channels)
    output = flat + jnp.dot(attended, w_out, preferred_element_type=jnp.float32)
    return output.astype(jnp.bfloat16).reshape(count, times, channels)

def reference(signal, lap_tiles, neighbours, cheb_weight, norm_gain, w_query, w_key, w_value, w_out):
    features = TIMES * C
    blocks = signal.reshape(NBLKS, B, features)
    first_order = laplace(lap_tiles, neighbours, blocks, None)
    second_order = laplace(lap_tiles, neighbours, first_order, blocks)

    def finish(index):
        plain = blocks[index].reshape(B * TIMES, C)
        one_term = first_order[index].reshape(B * TIMES, C)
        two_term = second_order[index].reshape(B * TIMES, C)
        mixing = jnp.dot(plain, cheb_weight[0], preferred_element_type=jnp.float32)
        mixing = mixing + jnp.dot(one_term, cheb_weight[1], preferred_element_type=jnp.float32)
        mixing = mixing + jnp.dot(two_term, cheb_weight[2], preferred_element_type=jnp.float32)
        mixed = (plain.astype(jnp.float32) + jax.nn.silu(mixing)).astype(jnp.bfloat16)
        return attend(mixed.reshape(B, TIMES, C), norm_gain, w_query, w_key, w_value, w_out)
    output = lax.map(finish, jnp.arange(NBLKS, dtype=jnp.int32))
    return output.reshape(PIX, TIMES, C)
```

```python
import math

import jax
import jax.numpy as jnp
from jax import lax
from jax.experimental import pallas as pl
from jax.experimental.pallas import tpu as pltpu
from jax.sharding import PartitionSpec as P

HEADS = 8
REACH = 2
GROUP = 8
MESH = pl.DeviceIdType.MESH
BF16 = jnp.bfloat16
F32 = jnp.float32


def matmul(left, right):
    return jnp.dot(left, right, preferred_element_type=F32)


def kernel(
    nbr_ref, x_ref, tiles_ref, cheb_ref, gain_ref, wq_ref, wk_ref, wv_ref, wo_ref, out_ref,
    band, first_buf, halo1, halo2, mixed_buf, gathered, back_send, back,
    h1_send, h1_recv, h2_send, h2_recv, a_send, a_recv, b_send, b_recv,
):
    pix_n, tm_n = lax.axis_size("pix"), lax.axis_size("tm")
    pix, tm = lax.axis_index("pix"), lax.axis_index("tm")
    right = lax.rem(pix + 1, pix_n)
    left = lax.rem(pix + pix_n - 1, pix_n)
    own_blocks, slots, tile, _ = tiles_ref.shape
    rows, features = x_ref.shape
    edge = REACH * tile
    channels = cheb_ref.shape[1]
    own_times = features // channels
    times = own_times * tm_n
    share = rows // tm_n

    barrier = pltpu.get_barrier_semaphore()
    for side in (left, right):
        pl.semaphore_signal(barrier, inc=1, device_id={"pix": side}, device_id_type=MESH)
    for k in range(1, tm_n):
        pl.semaphore_signal(
            barrier, inc=1, device_id={"tm": lax.rem(tm + k, tm_n)}, device_id_type=MESH
        )
    pl.semaphore_wait(barrier, 2 + tm_n - 1)

    def halo(source, target, send, recv):
        copies = []
        for at, (side, start, land) in enumerate(
            ((right, rows - edge, 0), (left, 0, edge))
        ):
            copies.append(
                pltpu.make_async_remote_copy(
                    src_ref=source.at[pl.ds(start, edge), :],
                    dst_ref=target.at[pl.ds(land, edge), :],
                    send_sem=send.at[at],
                    recv_sem=recv.at[at],
                    device_id={"pix": side},
                    device_id_type=MESH,
                )
            )
        for copy in copies:
            copy.start()
        return copies

    first_halo = halo(x_ref, halo1, h1_send, h1_recv)

    base = pix * own_blocks
    wide = own_blocks + 2 * REACH
    order = list(range(REACH, REACH + own_blocks)) + list(range(REACH)) + list(
        range(REACH + own_blocks, wide)
    )
    for g in range(own_blocks):
        spots = [nbr_ref[j, base + g] - base + REACH for j in range(slots)]
        held = [tiles_ref[g, j].astype(F32) for j in range(slots)]

        def entry(e):
            off = e - g
            if off < 0 or off > 2 * REACH:
                return jnp.zeros((tile, tile), F32)
            span = 2 * REACH + 1
            used = range(slots) if off == REACH else [off] + list(range(span, slots))
            total = None
            for j in used:
                term = held[j] * jnp.where(spots[j] == e, 1.0, 0.0).astype(F32)
                total = term if total is None else total + term
            return total

        for at in range(0, wide, 2):
            pair = jnp.concatenate([entry(order[at]), entry(order[at + 1])], axis=1)
            band[g * tile : (g + 1) * tile, at * tile : (at + 2) * tile] = pair.astype(BF16)

    signal = x_ref[...]
    own_first = matmul(band[:, :rows], signal)
    for copy in first_halo:
        copy.wait()
    first = (own_first + matmul(band[:, rows:], halo1[...])).astype(BF16)
    first_buf[...] = first
    second_halo = halo(first_buf, halo2, h2_send, h2_recv)

    own_second = matmul(band[:, :rows], first)
    partial = [
        matmul(signal[:, t * channels : (t + 1) * channels], cheb_ref[0])
        + matmul(first[:, t * channels : (t + 1) * channels], cheb_ref[1])
        for t in range(own_times)
    ]
    for copy in second_halo:
        copy.wait()
    wide_signal = signal.astype(F32)
    second = (
        2.0 * (own_second + matmul(band[:, rows:], halo2[...])) - wide_signal
    ).astype(BF16)
    for t in range(own_times):
        lanes = slice(t * channels, (t + 1) * channels)
        mixing = partial[t] + matmul(second[:, lanes], cheb_ref[2])
        mixed = wide_signal[:, lanes] + mixing / (1.0 + jnp.exp(-mixing))
        mixed_buf[:, lanes] = mixed.astype(BF16)

    out_copies = []
    for k in range(1, tm_n):
        peer = lax.rem(tm + k, tm_n)
        out_copies.append(
            pltpu.make_async_remote_copy(
                src_ref=mixed_buf.at[pl.ds(pl.multiple_of(peer * share, share), share), :],
                dst_ref=gathered.at[tm],
                send_sem=a_send.at[k - 1],
                recv_sem=a_recv.at[k - 1],
                device_id={"tm": peer},
                device_id_type=MESH,
            )
        )
    for copy in out_copies:
        copy.start()
    mine = pl.ds(pl.multiple_of(tm * share, share), share)
    gathered[tm] = mixed_buf[mine, :]
    for copy in out_copies:
        copy.wait()

    pieces = []
    for source in range(tm_n):
        piece = gathered[source].astype(F32)
        for t in range(own_times):
            pieces.append(piece[:, t * channels : (t + 1) * channels])
    flat = jnp.concatenate(pieces, axis=0)
    scaling = lax.rsqrt(jnp.mean(flat * flat, axis=1, keepdims=True) + 1e-06)
    normed = (flat * scaling * gain_ref[...]).astype(BF16)
    query = matmul(normed, wq_ref[...]).reshape(times, share, channels)
    keys = matmul(normed, wk_ref[...]).reshape(times, share, channels)
    values = matmul(normed, wv_ref[...]).reshape(times, share, channels)

    head_dim = channels // HEADS
    lane = lax.broadcasted_iota(jnp.int32, (1, channels), 1)
    head_masks = [
        jnp.where((lane >= h * head_dim) & (lane < (h + 1) * head_dim), 1.0, 0.0).astype(F32)
        for h in range(HEADS)
    ]
    count = times * GROUP
    row_pixel = lax.broadcasted_iota(jnp.int32, (HEADS * count, count), 0) & (GROUP - 1)
    col_pixel = lax.broadcasted_iota(jnp.int32, (HEADS * count, count), 1) & (GROUP - 1)
    same = row_pixel == col_pixel
    attended = []
    for group in range(share // GROUP):
        pick = slice(group * GROUP, (group + 1) * GROUP)
        q = query[:, pick].reshape(count, channels)
        k = keys[:, pick].reshape(count, channels).astype(BF16)
        v = values[:, pick].reshape(count, channels).astype(BF16)
        stacked = jnp.concatenate([(q * m).astype(BF16) for m in head_masks], axis=0)
        scores = lax.dot_general(
            stacked, k, (((1,), (1,)), ((), ())), preferred_element_type=F32
        ) * (1.0 / math.sqrt(head_dim))
        scores = jnp.where(same, scores, -jnp.inf)
        top = jnp.max(scores, axis=1, keepdims=True)
        weights = jnp.exp(scores - top)
        norm = jnp.sum(weights, axis=1, keepdims=True)
        product = matmul(weights.astype(BF16), v) / norm
        total = None
        for h in range(HEADS):
            term = product[h * count : (h + 1) * count] * head_masks[h]
            total = term if total is None else total + term
        attended.append(total.reshape(times, GROUP, channels))
    joined = jnp.concatenate(attended, axis=1).reshape(times * share, channels).astype(BF16)
    result = flat + matmul(joined, wo_ref[...])
    for t in range(times):
        lanes = slice((t % own_times) * channels, (t % own_times + 1) * channels)
        back_send[t // own_times, :, lanes] = result[t * share : (t + 1) * share].astype(BF16)

    back_copies = []
    for k in range(1, tm_n):
        peer = lax.rem(tm + k, tm_n)
        back_copies.append(
            pltpu.make_async_remote_copy(
                src_ref=back_send.at[peer],
                dst_ref=back.at[tm],
                send_sem=b_send.at[k - 1],
                recv_sem=b_recv.at[k - 1],
                device_id={"tm": peer},
                device_id_type=MESH,
            )
        )
    for copy in back_copies:
        copy.start()
    back[tm] = back_send[tm]
    for copy in back_copies:
        copy.wait()
    for source in range(tm_n):
        out_ref[source * share : (source + 1) * share, :] = back[source]


def on_device(
    signal, lap_tiles, neighbours, cheb_weight, norm_gain, w_query, w_key, w_value, w_out
):
    pix_count, time_count, channels = signal.shape
    tm_n = lax.axis_size("tm")
    tile = lap_tiles.shape[2]
    features = time_count * channels
    share = pix_count // tm_n
    halo_rows = 2 * REACH * tile
    vmem = pl.BlockSpec(memory_space=pltpu.VMEM)
    dma = pltpu.SemaphoreType.DMA
    out = pl.pallas_call(
        kernel,
        out_shape=jax.ShapeDtypeStruct((pix_count, features), BF16),
        in_specs=[pl.BlockSpec(memory_space=pltpu.SMEM)] + [vmem] * 8,
        out_specs=vmem,
        scratch_shapes=[
            pltpu.VMEM((pix_count, pix_count + halo_rows), BF16),
            pltpu.VMEM((pix_count, features), BF16),
            pltpu.VMEM((halo_rows, features), BF16),
            pltpu.VMEM((halo_rows, features), BF16),
            pltpu.VMEM((pix_count, features), BF16),
            pltpu.VMEM((tm_n, share, features), BF16),
            pltpu.VMEM((tm_n, share, features), BF16),
            pltpu.VMEM((tm_n, share, features), BF16),
            dma((2,)),
            dma((2,)),
            dma((2,)),
            dma((2,)),
            dma((tm_n - 1,)),
            dma((tm_n - 1,)),
            dma((tm_n - 1,)),
            dma((tm_n - 1,)),
        ],
        compiler_params=pltpu.CompilerParams(
            collective_id=0, has_side_effects=True, vmem_limit_bytes=48 << 20
        ),
        name="cheb_attend",
    )(
        neighbours.T,
        signal.reshape(pix_count, features),
        lap_tiles,
        cheb_weight,
        norm_gain.reshape(1, channels),
        w_query,
        w_key,
        w_value,
        w_out,
    )
    return out.reshape(pix_count, time_count, channels)


def solution(mesh):
    in_specs = (P("pix", "tm", None), P("pix", None, None, None), P(), P(), P(), P(), P(), P(), P())
    out_specs = P("pix", "tm", None)
    return jax.shard_map(
        on_device, mesh=mesh, in_specs=in_specs, out_specs=out_specs, check_vma=False
    )
```

```python
import math

import jax
import jax.numpy as jnp
from jax import lax
from jax.experimental import pallas as pl
from jax.experimental.pallas import tpu as pltpu
from jax.sharding import PartitionSpec as P

HEADS = 8
REACH = 2
GROUP = 8
CHUNKS = 2
MESH = pl.DeviceIdType.MESH
BF16 = jnp.bfloat16
F32 = jnp.float32


def matmul(left, right):
    return jnp.dot(left, right, preferred_element_type=F32)


def kernel(
    nbr_hbm, x_hbm, tiles_hbm, cheb_hbm, gain_hbm, wq_hbm, wk_hbm, wv_hbm, wo_hbm, out_ref,
    nbr_ref, x_ref, tiles_ref, cheb_ref, gain_ref, wq_ref, wk_ref, wv_ref, wo_ref,
    band, first_buf, halo1, halo2, mixed_buf, gathered, back_send, back,
    load_sem, h1_send, h1_recv, h2_send, h2_recv, a_send, a_recv, b_send, b_recv,
):
    pix_n, tm_n = lax.axis_size("pix"), lax.axis_size("tm")
    pix, tm = lax.axis_index("pix"), lax.axis_index("tm")
    right = lax.rem(pix + 1, pix_n)
    left = lax.rem(pix + pix_n - 1, pix_n)
    own_blocks, slots, tile, _ = tiles_ref.shape
    own_times, rows, channels = x_ref.shape
    edge = REACH * tile
    times = own_times * tm_n
    share = rows // tm_n
    part = share // CHUNKS

    loads = [
        pltpu.make_async_copy(source, target, load_sem.at[at])
        for at, (source, target) in enumerate(
            (
                (nbr_hbm, nbr_ref), (tiles_hbm, tiles_ref), (x_hbm, x_ref),
                (cheb_hbm, cheb_ref), (gain_hbm, gain_ref), (wq_hbm, wq_ref), (wk_hbm, wk_ref),
                (wv_hbm, wv_ref), (wo_hbm, wo_ref),
            )
        )
    ]
    for load in loads:
        load.start()

    barrier = pltpu.get_barrier_semaphore()
    for side in (left, right):
        pl.semaphore_signal(barrier, inc=1, device_id={"pix": side}, device_id_type=MESH)
    for k in range(1, tm_n):
        pl.semaphore_signal(
            barrier, inc=1, device_id={"tm": lax.rem(tm + k, tm_n)}, device_id_type=MESH
        )
    pl.semaphore_wait(barrier, 2 + tm_n - 1)

    sent = []

    def halo(source, target, send, recv, t):
        copies = []
        for at, (side, start, land) in enumerate(
            ((right, rows - edge, 0), (left, 0, edge))
        ):
            copies.append(
                pltpu.make_async_remote_copy(
                    src_ref=source.at[t, pl.ds(start, edge), :],
                    dst_ref=target.at[t, pl.ds(land, edge), :],
                    send_sem=send.at[t, at],
                    recv_sem=recv.at[t, at],
                    device_id={"pix": side},
                    device_id_type=MESH,
                )
            )
        for copy in copies:
            copy.start()
        sent.extend(copies)
        return copies

    first_halo = [halo(x_hbm, halo1, h1_send, h1_recv, t) for t in range(own_times)]

    loads[0].wait()
    loads[1].wait()
    base = pix * own_blocks
    wide = own_blocks + 2 * REACH
    order = list(range(REACH, REACH + own_blocks)) + list(range(REACH)) + list(
        range(REACH + own_blocks, wide)
    )
    for g in range(own_blocks):
        spots = [nbr_ref[j, base + g] - base + REACH for j in range(slots)]
        held = [tiles_ref[g, j].astype(F32) for j in range(slots)]

        def entry(e):
            off = e - g
            if off < 0 or off > 2 * REACH:
                return jnp.zeros((tile, tile), F32)
            span = 2 * REACH + 1
            used = range(slots) if off == REACH else [off] + list(range(span, slots))
            total = None
            for j in used:
                term = held[j] * jnp.where(spots[j] == e, 1.0, 0.0).astype(F32)
                total = term if total is None else total + term
            return total

        for at in range(0, wide, 2):
            pair = jnp.concatenate([entry(order[at]), entry(order[at + 1])], axis=1)
            band[g * tile : (g + 1) * tile, at * tile : (at + 2) * tile] = pair.astype(BF16)

    for load in loads[2:]:
        load.wait()
    own_first = [matmul(band[:, :rows], x_ref[t]) for t in range(own_times)]
    second_halo = []
    for t in range(own_times):
        for copy in first_halo[t]:
            copy.wait_recv()
        first_buf[t] = (own_first[t] + matmul(band[:, rows:], halo1[t])).astype(BF16)
        second_halo.append(halo(first_buf, halo2, h2_send, h2_recv, t))

    own_second = [matmul(band[:, :rows], first_buf[t]) for t in range(own_times)]
    partial = [
        matmul(x_ref[t], cheb_ref[0]) + matmul(first_buf[t], cheb_ref[1])
        for t in range(own_times)
    ]
    arriving = []
    for t in range(own_times):
        for copy in second_halo[t]:
            copy.wait_recv()
        wide_signal = x_ref[t].astype(F32)
        second = (
            2.0 * (own_second[t] + matmul(band[:, rows:], halo2[t])) - wide_signal
        ).astype(BF16)
        mixing = partial[t] + matmul(second, cheb_ref[2])
        mixed = wide_signal + mixing / (1.0 + jnp.exp(-mixing))
        mixed_buf[t] = mixed.astype(BF16)
        for c in range(CHUNKS):
            for k in range(1, tm_n):
                peer = lax.rem(tm + k, tm_n)
                start = pl.multiple_of(peer * share + c * part, part)
                copy = pltpu.make_async_remote_copy(
                    src_ref=mixed_buf.at[t, pl.ds(start, part), :],
                    dst_ref=gathered.at[c, tm, t],
                    send_sem=a_send.at[t, c, k - 1],
                    recv_sem=a_recv.at[t, c, k - 1],
                    device_id={"tm": peer},
                    device_id_type=MESH,
                )
                copy.start()
                arriving.append((c, copy))
                sent.append(copy)
        for c in range(CHUNKS):
            start = pl.multiple_of(tm * share + c * part, part)
            gathered[c, tm, t] = mixed_buf[t, pl.ds(start, part), :]

    head_dim = channels // HEADS
    lane = lax.broadcasted_iota(jnp.int32, (1, channels), 1)
    head_masks = [
        jnp.where((lane >= h * head_dim) & (lane < (h + 1) * head_dim), 1.0, 0.0).astype(F32)
        for h in range(HEADS)
    ]
    count = times * GROUP
    row_pixel = lax.broadcasted_iota(jnp.int32, (HEADS * count, count), 0) & (GROUP - 1)
    col_pixel = lax.broadcasted_iota(jnp.int32, (HEADS * count, count), 1) & (GROUP - 1)
    same = row_pixel == col_pixel
    returning = []
    for c in range(CHUNKS):
        for chunk, copy in arriving:
            if chunk == c:
                copy.wait_recv()
        flat = jnp.concatenate(
            [gathered[c, s, t].astype(F32) for s in range(tm_n) for t in range(own_times)],
            axis=0,
        )
        scaling = lax.rsqrt(jnp.mean(flat * flat, axis=1, keepdims=True) + 1e-06)
        normed = (flat * scaling * gain_ref[...]).astype(BF16)
        query = matmul(normed, wq_ref[...]).reshape(times, part, channels)
        keys = matmul(normed, wk_ref[...]).reshape(times, part, channels)
        values = matmul(normed, wv_ref[...]).reshape(times, part, channels)
        attended = []
        for group in range(part // GROUP):
            pick = slice(group * GROUP, (group + 1) * GROUP)
            q = query[:, pick].reshape(count, channels)
            k = keys[:, pick].reshape(count, channels).astype(BF16)
            v = values[:, pick].reshape(count, channels).astype(BF16)
            stacked = jnp.concatenate([(q * m).astype(BF16) for m in head_masks], axis=0)
            scores = lax.dot_general(
                stacked, k, (((1,), (1,)), ((), ())), preferred_element_type=F32
            ) * (1.0 / math.sqrt(head_dim))
            scores = jnp.where(same, scores, -jnp.inf)
            top = jnp.max(scores, axis=1, keepdims=True)
            weights = jnp.exp(scores - top)
            norm = jnp.sum(weights, axis=1, keepdims=True)
            product = matmul(weights.astype(BF16), v) / norm
            total = None
            for h in range(HEADS):
                term = product[h * count : (h + 1) * count] * head_masks[h]
                total = term if total is None else total + term
            attended.append(total.reshape(times, GROUP, channels))
        joined = jnp.concatenate(attended, axis=1).reshape(times * part, channels)
        result = flat + matmul(joined.astype(BF16), wo_ref[...])
        for t in range(times):
            back_send[c, t // own_times, t % own_times] = result[
                t * part : (t + 1) * part
            ].astype(BF16)
        for k in range(1, tm_n):
            peer = lax.rem(tm + k, tm_n)
            copy = pltpu.make_async_remote_copy(
                src_ref=back_send.at[c, peer],
                dst_ref=back.at[c, tm],
                send_sem=b_send.at[c, k - 1],
                recv_sem=b_recv.at[c, k - 1],
                device_id={"tm": peer},
                device_id_type=MESH,
            )
            copy.start()
            returning.append((c, copy))
            sent.append(copy)
        back[c, tm] = back_send[c, tm]

    for c in range(CHUNKS):
        for chunk, copy in returning:
            if chunk == c:
                copy.wait_recv()
        for s in range(tm_n):
            for t in range(own_times):
                start = s * share + c * part
                out_ref[t, start : start + part, :] = back[c, s, t]
    for copy in sent:
        copy.wait_send()


def on_device(
    signal, lap_tiles, neighbours, cheb_weight, norm_gain, w_query, w_key, w_value, w_out
):
    pix_count, time_count, channels = signal.shape
    tm_n = lax.axis_size("tm")
    tile = lap_tiles.shape[2]
    share = pix_count // tm_n
    part = share // CHUNKS
    halo_rows = 2 * REACH * tile
    vmem = pl.BlockSpec(memory_space=pltpu.VMEM)
    hbm = pl.BlockSpec(memory_space=pltpu.HBM)
    dma = pltpu.SemaphoreType.DMA
    operands = (
        neighbours.T,
        signal.transpose(1, 0, 2),
        lap_tiles,
        cheb_weight,
        norm_gain.reshape(1, channels),
        w_query,
        w_key,
        w_value,
        w_out,
    )
    local = [pltpu.SMEM(operands[0].shape, jnp.int32)] + [
        pltpu.VMEM(operand.shape, operand.dtype) for operand in operands[1:]
    ]
    slab = (time_count, pix_count, channels)
    halo_slab = (time_count, halo_rows, channels)
    exchange = (CHUNKS, tm_n, time_count, part, channels)
    out = pl.pallas_call(
        kernel,
        out_shape=jax.ShapeDtypeStruct(slab, BF16),
        in_specs=[hbm] * 9,
        out_specs=vmem,
        scratch_shapes=local
        + [
            pltpu.VMEM((pix_count, pix_count + halo_rows), BF16),
            pltpu.VMEM(slab, BF16),
            pltpu.VMEM(halo_slab, BF16),
            pltpu.VMEM(halo_slab, BF16),
            pltpu.VMEM(slab, BF16),
            pltpu.VMEM(exchange, BF16),
            pltpu.VMEM(exchange, BF16),
            pltpu.VMEM(exchange, BF16),
            dma((9,)),
        ]
        + [dma((time_count, 2))] * 4
        + [dma((time_count, CHUNKS, tm_n - 1))] * 2
        + [dma((CHUNKS, tm_n - 1))] * 2,
        compiler_params=pltpu.CompilerParams(
            collective_id=0, has_side_effects=True
        ),
        name="cheb_attend",
    )(*operands)
    return out.transpose(1, 0, 2)


def solution(mesh):
    in_specs = (P("pix", "tm", None), P("pix", None, None, None), P(), P(), P(), P(), P(), P(), P())
    out_specs = P("pix", "tm", None)
    return jax.shard_map(
        on_device, mesh=mesh, in_specs=in_specs, out_specs=out_specs, check_vma=False
    )
```

```python
import math

import jax
import jax.numpy as jnp
from jax import lax
from jax.experimental import pallas as pl
from jax.experimental.pallas import tpu as pltpu
from jax.sharding import PartitionSpec as P

HEADS = 8
REACH = 2
GROUP = 8
CHUNKS = 2
MESH = pl.DeviceIdType.MESH
BF16 = jnp.bfloat16
F32 = jnp.float32


def matmul(left, right):
    return jnp.dot(left, right, preferred_element_type=F32)


def kernel(
    nbr_hbm, x_hbm, tiles_hbm, cheb_hbm, gain_hbm, wq_hbm, wk_hbm, wv_hbm, wo_hbm, out_ref,
    nbr_ref, x_ref, tiles_ref, cheb_ref, gain_ref, wq_ref, wk_ref, wv_ref, wo_ref,
    band, first_buf, halo1, halo2, mixed_buf, gathered, back_send, back,
    load_sem, h1_send, h1_recv, h2_send, h2_recv, a_send, a_recv, b_send, b_recv,
):
    pix_n, tm_n = lax.axis_size("pix"), lax.axis_size("tm")
    pix, tm = lax.axis_index("pix"), lax.axis_index("tm")
    right = lax.rem(pix + 1, pix_n)
    left = lax.rem(pix + pix_n - 1, pix_n)
    own_blocks, slots, tile, _ = tiles_ref.shape
    own_times, rows, channels = x_ref.shape
    edge = REACH * tile
    times = own_times * tm_n
    share = rows // tm_n
    part = share // CHUNKS

    loads = [
        pltpu.make_async_copy(source, target, load_sem.at[at])
        for at, (source, target) in enumerate(
            (
                (nbr_hbm, nbr_ref), (tiles_hbm, tiles_ref), (x_hbm, x_ref),
                (cheb_hbm, cheb_ref), (gain_hbm, gain_ref), (wq_hbm, wq_ref), (wk_hbm, wk_ref),
                (wv_hbm, wv_ref), (wo_hbm, wo_ref),
            )
        )
    ]
    for load in loads:
        load.start()

    barrier = pltpu.get_barrier_semaphore()
    has_left, has_right = pix > 0, pix < pix_n - 1
    for side, present in ((left, has_left), (right, has_right)):

        @pl.when(present)
        def _():
            pl.semaphore_signal(barrier, inc=1, device_id={"pix": side}, device_id_type=MESH)

    for k in range(1, tm_n):
        pl.semaphore_signal(
            barrier, inc=1, device_id={"tm": lax.rem(tm + k, tm_n)}, device_id_type=MESH
        )
    present_count = jnp.minimum(pix, 1) + jnp.minimum(pix_n - 1 - pix, 1)
    pl.semaphore_wait(barrier, present_count + tm_n - 1)

    @pl.when(jnp.logical_not(has_left))
    def _():
        for buffer in (halo1, halo2):
            buffer[:, :edge] = jnp.zeros((own_times, edge, channels), BF16)

    @pl.when(jnp.logical_not(has_right))
    def _():
        for buffer in (halo1, halo2):
            buffer[:, edge:] = jnp.zeros((own_times, edge, channels), BF16)

    sent, halos = [], []

    def halo(source, target, send, recv, t):
        copies = []
        for at, (side, start, land) in enumerate(
            ((right, rows - edge, 0), (left, 0, edge))
        ):
            copies.append(
                pltpu.make_async_remote_copy(
                    src_ref=source.at[t, pl.ds(start, edge), :],
                    dst_ref=target.at[t, pl.ds(land, edge), :],
                    send_sem=send.at[t, at],
                    recv_sem=recv.at[t, at],
                    device_id={"pix": side},
                    device_id_type=MESH,
                )
            )
        pl.when(has_right)(copies[0].start)
        pl.when(has_left)(copies[1].start)
        halos.append(copies)
        return copies

    def halo_arrives(copies):
        pl.when(has_left)(copies[0].wait_recv)
        pl.when(has_right)(copies[1].wait_recv)

    first_halo = [halo(x_hbm, halo1, h1_send, h1_recv, t) for t in range(own_times)]

    loads[0].wait()
    loads[1].wait()
    base = pix * own_blocks
    wide = own_blocks + 2 * REACH
    order = list(range(REACH, REACH + own_blocks)) + list(range(REACH)) + list(
        range(REACH + own_blocks, wide)
    )
    for g in range(own_blocks):
        spots = [nbr_ref[j, base + g] - base + REACH for j in range(slots)]
        held = [tiles_ref[g, j].astype(F32) for j in range(slots)]

        def entry(e):
            off = e - g
            if off < 0 or off > 2 * REACH:
                return jnp.zeros((tile, tile), F32)
            span = 2 * REACH + 1
            used = range(slots) if off == REACH else [off] + list(range(span, slots))
            total = None
            for j in used:
                term = held[j] * jnp.where(spots[j] == e, 1.0, 0.0).astype(F32)
                total = term if total is None else total + term
            return total

        for at in range(0, wide, 2):
            pair = jnp.concatenate([entry(order[at]), entry(order[at + 1])], axis=1)
            band[g * tile : (g + 1) * tile, at * tile : (at + 2) * tile] = pair.astype(BF16)

    for load in loads[2:]:
        load.wait()
    own_first = [matmul(band[:, :rows], x_ref[t]) for t in range(own_times)]
    second_halo = []
    for t in range(own_times):
        halo_arrives(first_halo[t])
        first_buf[t] = (own_first[t] + matmul(band[:, rows:], halo1[t])).astype(BF16)
        second_halo.append(halo(first_buf, halo2, h2_send, h2_recv, t))

    own_second = [matmul(band[:, :rows], first_buf[t]) for t in range(own_times)]
    partial = [
        matmul(x_ref[t], cheb_ref[0]) + matmul(first_buf[t], cheb_ref[1])
        for t in range(own_times)
    ]
    arriving = []
    for t in range(own_times):
        halo_arrives(second_halo[t])
        wide_signal = x_ref[t].astype(F32)
        second = (
            2.0 * (own_second[t] + matmul(band[:, rows:], halo2[t])) - wide_signal
        ).astype(BF16)
        mixing = partial[t] + matmul(second, cheb_ref[2])
        mixed = wide_signal + mixing / (1.0 + jnp.exp(-mixing))
        mixed_buf[t] = mixed.astype(BF16)
        for c in range(CHUNKS):
            for k in range(1, tm_n):
                peer = lax.rem(tm + k, tm_n)
                start = pl.multiple_of(peer * share + c * part, part)
                copy = pltpu.make_async_remote_copy(
                    src_ref=mixed_buf.at[t, pl.ds(start, part), :],
                    dst_ref=gathered.at[c, tm, t],
                    send_sem=a_send.at[t, c, k - 1],
                    recv_sem=a_recv.at[t, c, k - 1],
                    device_id={"tm": peer},
                    device_id_type=MESH,
                )
                copy.start()
                arriving.append((c, copy))
                sent.append(copy)
        for c in range(CHUNKS):
            start = pl.multiple_of(tm * share + c * part, part)
            gathered[c, tm, t] = mixed_buf[t, pl.ds(start, part), :]

    head_dim = channels // HEADS
    lane = lax.broadcasted_iota(jnp.int32, (1, channels), 1)
    head_masks = [
        jnp.where((lane >= h * head_dim) & (lane < (h + 1) * head_dim), 1.0, 0.0).astype(F32)
        for h in range(HEADS)
    ]
    count = times * GROUP
    row_pixel = lax.broadcasted_iota(jnp.int32, (HEADS * count, count), 0) & (GROUP - 1)
    col_pixel = lax.broadcasted_iota(jnp.int32, (HEADS * count, count), 1) & (GROUP - 1)
    same = row_pixel == col_pixel
    returning = []
    for c in range(CHUNKS):
        for chunk, copy in arriving:
            if chunk == c:
                copy.wait_recv()
        flat = jnp.concatenate(
            [gathered[c, s, t].astype(F32) for s in range(tm_n) for t in range(own_times)],
            axis=0,
        )
        scaling = lax.rsqrt(jnp.mean(flat * flat, axis=1, keepdims=True) + 1e-06)
        normed = (flat * scaling * gain_ref[...]).astype(BF16)
        query = matmul(normed, wq_ref[...]).reshape(times, part, channels)
        keys = matmul(normed, wk_ref[...]).reshape(times, part, channels)
        values = matmul(normed, wv_ref[...]).reshape(times, part, channels)
        attended = []
        for group in range(part // GROUP):
            pick = slice(group * GROUP, (group + 1) * GROUP)
            q = query[:, pick].reshape(count, channels)
            k = keys[:, pick].reshape(count, channels).astype(BF16)
            v = values[:, pick].reshape(count, channels).astype(BF16)
            stacked = jnp.concatenate([(q * m).astype(BF16) for m in head_masks], axis=0)
            scores = lax.dot_general(
                stacked, k, (((1,), (1,)), ((), ())), preferred_element_type=F32
            ) * (1.0 / math.sqrt(head_dim))
            scores = jnp.where(same, scores, -jnp.inf)
            top = jnp.max(scores, axis=1, keepdims=True)
            weights = jnp.exp(scores - top)
            norm = jnp.sum(weights, axis=1, keepdims=True)
            product = matmul(weights.astype(BF16), v) / norm
            total = None
            for h in range(HEADS):
                term = product[h * count : (h + 1) * count] * head_masks[h]
                total = term if total is None else total + term
            attended.append(total.reshape(times, GROUP, channels))
        joined = jnp.concatenate(attended, axis=1).reshape(times * part, channels)
        result = flat + matmul(joined.astype(BF16), wo_ref[...])
        for t in range(times):
            back_send[c, t // own_times, t % own_times] = result[
                t * part : (t + 1) * part
            ].astype(BF16)
        for k in range(1, tm_n):
            peer = lax.rem(tm + k, tm_n)
            copy = pltpu.make_async_remote_copy(
                src_ref=back_send.at[c, peer],
                dst_ref=back.at[c, tm],
                send_sem=b_send.at[c, k - 1],
                recv_sem=b_recv.at[c, k - 1],
                device_id={"tm": peer},
                device_id_type=MESH,
            )
            copy.start()
            returning.append((c, copy))
            sent.append(copy)
        back[c, tm] = back_send[c, tm]

    for c in range(CHUNKS):
        for chunk, copy in returning:
            if chunk == c:
                copy.wait_recv()
        for s in range(tm_n):
            for t in range(own_times):
                start = s * share + c * part
                out_ref[t, start : start + part, :] = back[c, s, t]
    for to_right, to_left in halos:
        pl.when(has_right)(to_right.wait_send)
        pl.when(has_left)(to_left.wait_send)
    for copy in sent:
        copy.wait_send()


def on_device(
    signal, lap_tiles, neighbours, cheb_weight, norm_gain, w_query, w_key, w_value, w_out
):
    pix_count, time_count, channels = signal.shape
    tm_n = lax.axis_size("tm")
    tile = lap_tiles.shape[2]
    share = pix_count // tm_n
    part = share // CHUNKS
    halo_rows = 2 * REACH * tile
    vmem = pl.BlockSpec(memory_space=pltpu.VMEM)
    hbm = pl.BlockSpec(memory_space=pltpu.HBM)
    dma = pltpu.SemaphoreType.DMA
    operands = (
        neighbours.T,
        signal.transpose(1, 0, 2),
        lap_tiles,
        cheb_weight,
        norm_gain.reshape(1, channels),
        w_query,
        w_key,
        w_value,
        w_out,
    )
    local = [pltpu.SMEM(operands[0].shape, jnp.int32)] + [
        pltpu.VMEM(operand.shape, operand.dtype) for operand in operands[1:]
    ]
    slab = (time_count, pix_count, channels)
    halo_slab = (time_count, halo_rows, channels)
    exchange = (CHUNKS, tm_n, time_count, part, channels)
    out = pl.pallas_call(
        kernel,
        out_shape=jax.ShapeDtypeStruct(slab, BF16),
        in_specs=[hbm] * 9,
        out_specs=vmem,
        scratch_shapes=local
        + [
            pltpu.VMEM((pix_count, pix_count + halo_rows), BF16),
            pltpu.VMEM(slab, BF16),
            pltpu.VMEM(halo_slab, BF16),
            pltpu.VMEM(halo_slab, BF16),
            pltpu.VMEM(slab, BF16),
            pltpu.VMEM(exchange, BF16),
            pltpu.VMEM(exchange, BF16),
            pltpu.VMEM(exchange, BF16),
            dma((9,)),
        ]
        + [dma((time_count, 2))] * 4
        + [dma((time_count, CHUNKS, tm_n - 1))] * 2
        + [dma((CHUNKS, tm_n - 1))] * 2,
        compiler_params=pltpu.CompilerParams(
            collective_id=0, has_side_effects=True
        ),
        name="cheb_attend",
    )(*operands)
    return out.transpose(1, 0, 2)


def solution(mesh):
    in_specs = (P("pix", "tm", None), P("pix", None, None, None), P(), P(), P(), P(), P(), P(), P())
    out_specs = P("pix", "tm", None)
    return jax.shard_map(
        on_device, mesh=mesh, in_specs=in_specs, out_specs=out_specs, check_vma=False
    )
```

```python
import math

import jax
import jax.numpy as jnp
from jax import lax
from jax.experimental import pallas as pl
from jax.experimental.pallas import tpu as pltpu
from jax.sharding import PartitionSpec as P

HEADS = 8
REACH = 2
GROUP = 8
CHUNKS = 2
MESH = pl.DeviceIdType.MESH
BF16 = jnp.bfloat16
F32 = jnp.float32


def matmul(left, right):
    return jnp.dot(left, right, preferred_element_type=F32)


def kernel(
    nbr_hbm, x_hbm, tiles_hbm, cheb_hbm, gain_hbm, wq_hbm, wk_hbm, wv_hbm, wo_hbm, out_ref,
    nbr_ref, x_pairs, tiles_ref, cheb_ref, gain_ref, wq_ref, wk_ref, wv_ref, wo_ref,
    x_ref, band, first_buf, halo1, halo2, mixed_buf, gathered, back_send, back,
    load_sem, h1_send, h1_recv, h2_send, h2_recv, a_send, a_recv, b_send, b_recv,
):
    pix_n, tm_n = lax.axis_size("pix"), lax.axis_size("tm")
    pix, tm = lax.axis_index("pix"), lax.axis_index("tm")
    right = lax.rem(pix + 1, pix_n)
    left = lax.rem(pix + pix_n - 1, pix_n)
    own_blocks, slots, tile, _ = tiles_ref.shape
    own_times, rows, channels = x_ref.shape
    edge = REACH * tile
    times = own_times * tm_n
    share = rows // tm_n
    part = share // CHUNKS

    loads = [
        pltpu.make_async_copy(source, target, load_sem.at[at])
        for at, (source, target) in enumerate(
            (
                (x_hbm, x_pairs), (nbr_hbm, nbr_ref), (tiles_hbm, tiles_ref),
                (cheb_hbm, cheb_ref), (gain_hbm, gain_ref), (wq_hbm, wq_ref), (wk_hbm, wk_ref),
                (wv_hbm, wv_ref), (wo_hbm, wo_ref),
            )
        )
    ]
    for load in loads:
        load.start()

    barrier = pltpu.get_barrier_semaphore()
    has_left, has_right = pix > 0, pix < pix_n - 1
    for side, present in ((left, has_left), (right, has_right)):

        @pl.when(present)
        def _():
            pl.semaphore_signal(barrier, inc=1, device_id={"pix": side}, device_id_type=MESH)

    for k in range(1, tm_n):
        pl.semaphore_signal(
            barrier, inc=1, device_id={"tm": lax.rem(tm + k, tm_n)}, device_id_type=MESH
        )
    loads[0].wait()
    for t in range(own_times):
        x_ref[t] = x_pairs[:, t, :]
    present_count = jnp.minimum(pix, 1) + jnp.minimum(pix_n - 1 - pix, 1)
    pl.semaphore_wait(barrier, present_count + tm_n - 1)

    @pl.when(jnp.logical_not(has_left))
    def _():
        for buffer in (halo1, halo2):
            buffer[:, :edge] = jnp.zeros((own_times, edge, channels), BF16)

    @pl.when(jnp.logical_not(has_right))
    def _():
        for buffer in (halo1, halo2):
            buffer[:, edge:] = jnp.zeros((own_times, edge, channels), BF16)

    sent, halos = [], []

    def halo(source, target, send, recv, t):
        copies = []
        for at, (side, start, land) in enumerate(
            ((right, rows - edge, 0), (left, 0, edge))
        ):
            copies.append(
                pltpu.make_async_remote_copy(
                    src_ref=source.at[t, pl.ds(start, edge), :],
                    dst_ref=target.at[t, pl.ds(land, edge), :],
                    send_sem=send.at[t, at],
                    recv_sem=recv.at[t, at],
                    device_id={"pix": side},
                    device_id_type=MESH,
                )
            )
        pl.when(has_right)(copies[0].start)
        pl.when(has_left)(copies[1].start)
        halos.append(copies)
        return copies

    def halo_arrives(copies):
        pl.when(has_left)(copies[0].wait_recv)
        pl.when(has_right)(copies[1].wait_recv)

    first_halo = [halo(x_ref, halo1, h1_send, h1_recv, t) for t in range(own_times)]

    loads[1].wait()
    loads[2].wait()
    base = pix * own_blocks
    wide = own_blocks + 2 * REACH
    order = list(range(REACH, REACH + own_blocks)) + list(range(REACH)) + list(
        range(REACH + own_blocks, wide)
    )
    for g in range(own_blocks):
        spots = [nbr_ref[j, base + g] - base + REACH for j in range(slots)]
        held = [tiles_ref[g, j].astype(F32) for j in range(slots)]

        def entry(e):
            off = e - g
            if off < 0 or off > 2 * REACH:
                return jnp.zeros((tile, tile), F32)
            span = 2 * REACH + 1
            used = range(slots) if off == REACH else [off] + list(range(span, slots))
            total = None
            for j in used:
                term = held[j] * jnp.where(spots[j] == e, 1.0, 0.0).astype(F32)
                total = term if total is None else total + term
            return total

        for at in range(0, wide, 2):
            pair = jnp.concatenate([entry(order[at]), entry(order[at + 1])], axis=1)
            band[g * tile : (g + 1) * tile, at * tile : (at + 2) * tile] = pair.astype(BF16)

    for load in loads[3:]:
        load.wait()
    own_first = [matmul(band[:, :rows], x_ref[t]) for t in range(own_times)]
    second_halo = []
    for t in range(own_times):
        halo_arrives(first_halo[t])
        first_buf[t] = (own_first[t] + matmul(band[:, rows:], halo1[t])).astype(BF16)
        second_halo.append(halo(first_buf, halo2, h2_send, h2_recv, t))

    own_second = [matmul(band[:, :rows], first_buf[t]) for t in range(own_times)]
    partial = [
        matmul(x_ref[t], cheb_ref[0]) + matmul(first_buf[t], cheb_ref[1])
        for t in range(own_times)
    ]
    arriving = []
    for t in range(own_times):
        halo_arrives(second_halo[t])
        wide_signal = x_ref[t].astype(F32)
        second = (
            2.0 * (own_second[t] + matmul(band[:, rows:], halo2[t])) - wide_signal
        ).astype(BF16)
        mixing = partial[t] + matmul(second, cheb_ref[2])
        mixed = wide_signal + mixing / (1.0 + jnp.exp(-mixing))
        mixed_buf[t] = mixed.astype(BF16)
        for c in range(CHUNKS):
            for k in range(1, tm_n):
                peer = lax.rem(tm + k, tm_n)
                start = pl.multiple_of(peer * share + c * part, part)
                copy = pltpu.make_async_remote_copy(
                    src_ref=mixed_buf.at[t, pl.ds(start, part), :],
                    dst_ref=gathered.at[c, tm, t],
                    send_sem=a_send.at[t, c, k - 1],
                    recv_sem=a_recv.at[t, c, k - 1],
                    device_id={"tm": peer},
                    device_id_type=MESH,
                )
                copy.start()
                arriving.append((c, copy))
                sent.append(copy)
        for c in range(CHUNKS):
            start = pl.multiple_of(tm * share + c * part, part)
            gathered[c, tm, t] = mixed_buf[t, pl.ds(start, part), :]

    head_dim = channels // HEADS
    lane = lax.broadcasted_iota(jnp.int32, (1, channels), 1)
    head_masks = [
        jnp.where((lane >= h * head_dim) & (lane < (h + 1) * head_dim), 1.0, 0.0).astype(F32)
        for h in range(HEADS)
    ]
    count = times * GROUP
    row_pixel = lax.broadcasted_iota(jnp.int32, (HEADS * count, count), 0) & (GROUP - 1)
    col_pixel = lax.broadcasted_iota(jnp.int32, (HEADS * count, count), 1) & (GROUP - 1)
    same = row_pixel == col_pixel
    returning = []
    for c in range(CHUNKS):
        for chunk, copy in arriving:
            if chunk == c:
                copy.wait_recv()
        flat = jnp.concatenate(
            [gathered[c, s, t].astype(F32) for s in range(tm_n) for t in range(own_times)],
            axis=0,
        )
        scaling = lax.rsqrt(jnp.mean(flat * flat, axis=1, keepdims=True) + 1e-06)
        normed = (flat * scaling * gain_ref[...]).astype(BF16)
        query = matmul(normed, wq_ref[...]).reshape(times, part, channels)
        keys = matmul(normed, wk_ref[...]).reshape(times, part, channels)
        values = matmul(normed, wv_ref[...]).reshape(times, part, channels)
        attended = []
        for group in range(part // GROUP):
            pick = slice(group * GROUP, (group + 1) * GROUP)
            q = query[:, pick].reshape(count, channels)
            k = keys[:, pick].reshape(count, channels).astype(BF16)
            v = values[:, pick].reshape(count, channels).astype(BF16)
            stacked = jnp.concatenate([(q * m).astype(BF16) for m in head_masks], axis=0)
            scores = lax.dot_general(
                stacked, k, (((1,), (1,)), ((), ())), preferred_element_type=F32
            ) * (1.0 / math.sqrt(head_dim))
            scores = jnp.where(same, scores, -jnp.inf)
            top = jnp.max(scores, axis=1, keepdims=True)
            weights = jnp.exp(scores - top)
            norm = jnp.sum(weights, axis=1, keepdims=True)
            product = matmul(weights.astype(BF16), v) / norm
            total = None
            for h in range(HEADS):
                term = product[h * count : (h + 1) * count] * head_masks[h]
                total = term if total is None else total + term
            attended.append(total.reshape(times, GROUP, channels))
        joined = jnp.concatenate(attended, axis=1).reshape(times * part, channels)
        result = flat + matmul(joined.astype(BF16), wo_ref[...])
        for t in range(times):
            back_send[c, t // own_times, t % own_times] = result[
                t * part : (t + 1) * part
            ].astype(BF16)
        for k in range(1, tm_n):
            peer = lax.rem(tm + k, tm_n)
            copy = pltpu.make_async_remote_copy(
                src_ref=back_send.at[c, peer],
                dst_ref=back.at[c, tm],
                send_sem=b_send.at[c, k - 1],
                recv_sem=b_recv.at[c, k - 1],
                device_id={"tm": peer},
                device_id_type=MESH,
            )
            copy.start()
            returning.append((c, copy))
            sent.append(copy)
        back[c, tm] = back_send[c, tm]

    for c in range(CHUNKS):
        for chunk, copy in returning:
            if chunk == c:
                copy.wait_recv()
        for s in range(tm_n):
            for t in range(own_times):
                start = s * share + c * part
                out_ref[t, start : start + part, :] = back[c, s, t]
    for to_right, to_left in halos:
        pl.when(has_right)(to_right.wait_send)
        pl.when(has_left)(to_left.wait_send)
    for copy in sent:
        copy.wait_send()


def on_device(
    signal, lap_tiles, neighbours, cheb_weight, norm_gain, w_query, w_key, w_value, w_out
):
    pix_count, time_count, channels = signal.shape
    tm_n = lax.axis_size("tm")
    tile = lap_tiles.shape[2]
    share = pix_count // tm_n
    part = share // CHUNKS
    halo_rows = 2 * REACH * tile
    vmem = pl.BlockSpec(memory_space=pltpu.VMEM)
    hbm = pl.BlockSpec(memory_space=pltpu.HBM)
    dma = pltpu.SemaphoreType.DMA
    operands = (
        neighbours.T,
        signal,
        lap_tiles,
        cheb_weight,
        norm_gain.reshape(1, channels),
        w_query,
        w_key,
        w_value,
        w_out,
    )
    local = [pltpu.SMEM(operands[0].shape, jnp.int32)] + [
        pltpu.VMEM(operand.shape, operand.dtype) for operand in operands[1:]
    ]
    slab = (time_count, pix_count, channels)
    halo_slab = (time_count, halo_rows, channels)
    exchange = (CHUNKS, tm_n, time_count, part, channels)
    out = pl.pallas_call(
        kernel,
        out_shape=jax.ShapeDtypeStruct(slab, BF16),
        in_specs=[hbm] * 9,
        out_specs=vmem,
        scratch_shapes=local
        + [
            pltpu.VMEM(slab, BF16),
            pltpu.VMEM((pix_count, pix_count + halo_rows), BF16),
            pltpu.VMEM(slab, BF16),
            pltpu.VMEM(halo_slab, BF16),
            pltpu.VMEM(halo_slab, BF16),
            pltpu.VMEM(slab, BF16),
            pltpu.VMEM(exchange, BF16),
            pltpu.VMEM(exchange, BF16),
            pltpu.VMEM(exchange, BF16),
            dma((9,)),
        ]
        + [dma((time_count, 2))] * 4
        + [dma((time_count, CHUNKS, tm_n - 1))] * 2
        + [dma((CHUNKS, tm_n - 1))] * 2,
        compiler_params=pltpu.CompilerParams(
            collective_id=0, has_side_effects=True
        ),
        name="cheb_attend",
    )(*operands)
    return out.transpose(1, 0, 2)


def solution(mesh):
    in_specs = (P("pix", "tm", None), P("pix", None, None, None), P(), P(), P(), P(), P(), P(), P())
    out_specs = P("pix", "tm", None)
    return jax.shard_map(
        on_device, mesh=mesh, in_specs=in_specs, out_specs=out_specs, check_vma=False
    )
```
